32 devices in a mesh: bucket: 8 (over y, x, core), rel: 4 (over z).
Axes of the slice: x: 2, y: 2, z: 4, core: 2. Of those that a mesh axis runs over, the one named last changes fastest.
Arguments:
- src_feat: bfloat16 [2048, 768], P(('bucket', 'rel')), may hold values from -22 to 22
- tgt_feat: bfloat16 [4096, 768], P(('bucket', 'rel')), may hold values from -22 to 22
- enc_weight: bfloat16 [768, 512], replicated, may hold values from -0.21875 to 0.21875
- rel_shift: bfloat16 [12, 512], P('rel'), may hold values from -3 to 3
- edge_src: int32 [8, 4, 4, 768], P('bucket', 'rel'), may hold values from 0 to 255
- edge_tgt: int32 [8, 4, 4, 768], P('bucket', 'rel'), may hold values from 0 to 511
- rel_hot: int32 [8, 4, 4, 3, 768], P('bucket', 'rel'), may hold values from 0 to 1, as said below
- neg_idx: int32 [8, 4, 4, 128], P('bucket', 'rel'), may hold values from 0 to 511
- edge_label: int32 [8, 4, 4, 768], P('bucket', 'rel'), may hold values 0 or 1
Outputs:
- src_grad: float32 [2048, 512], P(('bucket', 'rel'))
- tgt_grad: float32 [4096, 512], P(('bucket', 'rel'))
- rel_grad: float32 [12, 512], P('rel')
- enc_grad: float32 [768, 512], replicated
The draws below stay inside these ranges and needn't reach their ends.
Inputs may be any that keep to these rules, and one draw needn't show every extreme that they name: `rel_hot`: for each edge exactly one of the three entries is 1.
All inputs are finite; a program needn't handle non-finite values. No bound on the sum of `edge_label` on one device may be relied on, other than what follows from the above.
Results may differ from the reference program's by a relative error of at most 0.00065.
The reference program's roundings to bfloat16 on the way (of `src_emb`, `tgt_emb` and `query`) count: a program that leaves them out, or rounds other values in their place, can miss the bound.
Values may be sent and summed in bfloat16 or wider, within the bound.
No kernel may reach another device: no remote copies, remote signals or barrier semaphores. Data moves between devices by JAX's collectives and lax.ppermute only.
A program may use at most 64 MiB of HBM per device.

```python
import jax
import jax.numpy as jnp
from jax import lax

F = 768
EMB = 512
SRC_DEV = 256
TGT_DEV = 512
EDGES = 768
NEG = 128
MEETS = 4
BUCKETS = 8
GROUPS = 4
NSRC = 2048
NTGT = 4096


def draw_rel_hot(key, part):
    which = jax.random.randint(jax.random.fold_in(key, 17), (BUCKETS, GROUPS, MEETS, EDGES), 0, 3)
    levels = jnp.arange(3, dtype=jnp.int32)
    return (which[:, :, :, None, :] == levels[None, None, None, :, None]).astype(jnp.int32)


def shared_directions(key):
    base = jax.random.fold_in(key, 7)
    return jnp.clip(jax.random.normal(base, (2, F), jnp.float32), -3.0, 3.0)


def block_spike(key, row_count, salt):
    block_count = BUCKETS * GROUPS
    rows_block = row_count // block_count
    columns = jax.random.randint(jax.random.fold_in(key, salt + 100), (block_count,), 0, F)
    picked = (columns[:, None] == jnp.arange(F, dtype=jnp.int32)[None, :]).astype(jnp.float32)
    factor = 1.0 + 2.0 * picked
    return jnp.repeat(factor, rows_block, axis=0)


def node_features(key, row_count, salt):
    directions = shared_directions(key)
    node_key = jax.random.fold_in(key, salt)
    key_noise, key_coef = jax.random.split(node_key, 2)
    noise = jnp.clip(jax.random.normal(key_noise, (row_count, F), jnp.float32), -4.0, 4.0)
    coef = 0.5 * jnp.clip(jax.random.normal(key_coef, (row_count, 2), jnp.float32), -3.0, 3.0)
    feats = noise + coef[:, 0:1] * directions[0][None, :] + coef[:, 1:2] * directions[1][None, :]
    feats = feats * block_spike(key, row_count, salt)
    return feats.astype(jnp.bfloat16)


def draw_src_feat(key, part):
    return node_features(key, NSRC, 11)


def draw_tgt_feat(key, part):
    return node_features(key, NTGT, 13)


def place_ends(entries, stream_key, least, high):
    place = [jax.random.randint(jax.random.fold_in(stream_key, axis), (), 0, length) for axis, length in enumerate(entries.shape)]
    longest = entries.shape.index(max(entries.shape))
    neighbour = place[:longest] + [(place[longest] + 1) % entries.shape[longest]] + place[longest + 1:]
    return entries.at[tuple(place)].set(least).at[tuple(neighbour)].set(high)


def steps_of(key, extent, pieces, smallest, top_value):
    gain, own = 1.0, jax.random.fold_in(key, 6)
    for dim, blocks in pieces:
        heights = jnp.exp(jax.random.uniform(jax.random.fold_in(own, dim), (blocks,), jnp.float32, smallest / len(pieces), top_value / len(pieces)))
        gain = gain * jnp.repeat(heights, extent[dim] // blocks).reshape([-1 if axis == dim else 1 for axis in range(len(extent))])
    return gain


def centred(stream_key, shape, scale, limit, cuts=(), kind=jnp.bfloat16):
    gain = steps_of(stream_key, shape, cuts, -0.22, 0.18) if cuts else 1.0
    entries = jax.random.normal(stream_key, shape, jnp.float32) * scale * gain
    return jnp.minimum(jnp.maximum(entries, -limit), limit).astype(kind)


def setup_inputs(seed: int = 0) -> dict:
    splits = jax.random.split(jax.random.key(seed), 10)
    src_feat = draw_src_feat(jax.random.fold_in(splits[9], 71), 0)
    tgt_feat = draw_tgt_feat(jax.random.fold_in(splits[9], 71), 0)
    enc_weight = centred(splits[2], (F, EMB), F ** -0.5, 0.21875)
    rel_shift = centred(splits[3], (GROUPS * 3, EMB), 0.5, 3.0, ((0, 4),))
    edge_src = place_ends(jax.random.randint(splits[4], (BUCKETS, GROUPS, MEETS, EDGES), 0, SRC_DEV), jax.random.fold_in(splits[4], 1), 0, SRC_DEV - 1).astype(jnp.int32)
    edge_tgt = place_ends(jax.random.randint(splits[5], (BUCKETS, GROUPS, MEETS, EDGES), 0, TGT_DEV), jax.random.fold_in(splits[5], 1), 0, TGT_DEV - 1).astype(jnp.int32)
    rel_hot = draw_rel_hot(jax.random.fold_in(splits[9], 71), 0)
    neg_idx = place_ends(jax.random.randint(splits[7], (BUCKETS, GROUPS, MEETS, NEG), 0, TGT_DEV), jax.random.fold_in(splits[7], 1), 0, TGT_DEV - 1).astype(jnp.int32)
    edge_label = place_ends((jax.random.randint(splits[8], (BUCKETS, GROUPS, MEETS, EDGES), 0, 2) < 1).astype(jnp.int32), jax.random.fold_in(splits[8], 1), 0, 1)
    return dict(src_feat=src_feat, tgt_feat=tgt_feat, enc_weight=enc_weight, rel_shift=rel_shift, edge_src=edge_src, edge_tgt=edge_tgt, rel_hot=rel_hot, neg_idx=neg_idx, edge_label=edge_label)


def meet(source, block, shifts, src_ids, tgt_ids, hot, neg_ids, label):
    scale = EMB ** -0.5
    hot_b = hot.astype(jnp.bfloat16)
    shift = jnp.einsum("ke,kd->ed", hot_b, shifts, preferred_element_type=jnp.float32)
    query = (source[src_ids].astype(jnp.float32) + shift).astype(jnp.bfloat16)
    query_f = query.astype(jnp.float32)
    pos_rows = block[tgt_ids]
    neg_rows = block[neg_ids]
    pos = scale * jnp.sum(query_f * pos_rows.astype(jnp.float32), axis=1)
    neg = scale * jnp.einsum("ed,nd->en", query, neg_rows, preferred_element_type=jnp.float32)
    grad_pos = jax.nn.sigmoid(pos) - label.astype(jnp.float32)
    grad_neg = (jax.nn.sigmoid(neg) / NEG).astype(jnp.bfloat16)
    d_query = scale * (grad_pos[:, None] * pos_rows.astype(jnp.float32)
                       + jnp.einsum("en,nd->ed", grad_neg, neg_rows, preferred_element_type=jnp.float32))
    src_part = jnp.zeros((source.shape[0], EMB), jnp.float32).at[src_ids].add(d_query)
    tgt_part = jnp.zeros((block.shape[0], EMB), jnp.float32).at[tgt_ids].add(scale * grad_pos[:, None] * query_f)
    tgt_part = tgt_part.at[neg_ids].add(scale * jnp.einsum("en,ed->nd", grad_neg, query, preferred_element_type=jnp.float32))
    rel_part = jnp.einsum("ke,ed->kd", hot.astype(jnp.float32), d_query, precision=lax.Precision.HIGHEST)
    return src_part, tgt_part, rel_part


def reference(src_feat, tgt_feat, enc_weight, rel_shift, edge_src, edge_tgt, rel_hot, neg_idx, edge_label):
    src_act = jnp.tanh(jnp.dot(src_feat, enc_weight, preferred_element_type=jnp.float32))
    tgt_act = jnp.tanh(jnp.dot(tgt_feat, enc_weight, preferred_element_type=jnp.float32))
    src_emb = src_act.astype(jnp.bfloat16)
    tgt_emb = tgt_act.astype(jnp.bfloat16)
    half = BUCKETS // 2
    masks = [0, 1, 1 + half, half]

    def one_pair(flat, carry):
        src_total, tgt_total, rel_total = carry
        bucket = flat // GROUPS
        group = flat % GROUPS
        source = lax.dynamic_slice_in_dim(src_emb, (bucket * SRC_DEV).astype(jnp.int32), SRC_DEV, 0)
        shifts = lax.dynamic_slice_in_dim(rel_shift, (group * 3).astype(jnp.int32), 3, 0)
        src_sum = jnp.zeros((SRC_DEV, EMB), jnp.float32)
        rel_sum = jnp.zeros((3, EMB), jnp.float32)
        for slot in range(MEETS):
            partner = jnp.bitwise_xor(bucket, masks[slot]).astype(jnp.int32)
            block = lax.dynamic_slice_in_dim(tgt_emb, partner * TGT_DEV, TGT_DEV, 0)
            src_part, tgt_part, rel_part = meet(source, block, shifts, edge_src[bucket, group, slot],
                                               edge_tgt[bucket, group, slot], rel_hot[bucket, group, slot],
                                               neg_idx[bucket, group, slot], edge_label[bucket, group, slot])
            src_sum = src_sum + src_part
            rel_sum = rel_sum + rel_part
            old = lax.dynamic_slice_in_dim(tgt_total, partner * TGT_DEV, TGT_DEV, 0)
            tgt_total = lax.dynamic_update_slice_in_dim(tgt_total, old + tgt_part, partner * TGT_DEV, 0)
        old_src = lax.dynamic_slice_in_dim(src_total, (bucket * SRC_DEV).astype(jnp.int32), SRC_DEV, 0)
        src_total = lax.dynamic_update_slice_in_dim(src_total, old_src + src_sum, (bucket * SRC_DEV).astype(jnp.int32), 0)
        old_rel = lax.dynamic_slice_in_dim(rel_total, (group * 3).astype(jnp.int32), 3, 0)
        rel_total = lax.dynamic_update_slice_in_dim(rel_total, old_rel + rel_sum, (group * 3).astype(jnp.int32), 0)
        return src_total, tgt_total, rel_total

    start = (jnp.zeros((NSRC, EMB), jnp.float32), jnp.zeros((NTGT, EMB), jnp.float32),
             jnp.zeros((GROUPS * 3, EMB), jnp.float32))
    src_grad, tgt_grad, rel_grad = lax.fori_loop(0, BUCKETS * GROUPS, one_pair, start)
    d_src = (src_grad * (1.0 - src_act * src_act)).astype(jnp.bfloat16)
    d_tgt = (tgt_grad * (1.0 - tgt_act * tgt_act)).astype(jnp.bfloat16)
    enc_grad = (jnp.einsum("rf,re->fe", src_feat, d_src, preferred_element_type=jnp.float32)
                + jnp.einsum("rf,re->fe", tgt_feat, d_tgt, preferred_element_type=jnp.float32))
    return src_grad, tgt_grad, rel_grad, enc_grad
```

```python
import functools

import jax
import jax.numpy as jnp
from jax import lax
from jax.experimental import pallas as pl
from jax.experimental.pallas import tpu as pltpu
from jax.sharding import PartitionSpec as P


LABELLED = 1024.0
LOG2E = 1.4426950408889634
SLOT_OF = (0, 1, 3, 2)
APART = (0, 2, 1, 3)
NT = (((1,), (1,)), ((), ()))
NN = (((1,), (0,)), ((), ()))
F32 = jnp.float32
BF16 = jnp.bfloat16
VMEM = pl.BlockSpec(memory_space=pltpu.VMEM)
ANY = pl.BlockSpec(memory_space=pl.ANY)


def dot(a, b, dims):
    return lax.dot_general(a, b, dims, preferred_element_type=F32)


def call(body, outs, ins, in_specs=None, scratch=(), flops=0):
    moved = sum(x.size * x.dtype.itemsize for x in ins)
    moved += sum(o.size * o.dtype.itemsize for o in outs)
    return pl.pallas_call(
        body,
        out_shape=tuple(outs),
        in_specs=in_specs or [VMEM] * len(ins),
        out_specs=tuple(VMEM for _ in outs),
        scratch_shapes=scratch,
        cost_estimate=pl.CostEstimate(flops=int(flops), bytes_accessed=int(moved), transcendentals=0),
    )(*ins)


def shaped(shape, dtype=F32):
    return jax.ShapeDtypeStruct(tuple(shape), dtype)


def field_starts(edges, negs):
    starts, at = {}, 0
    for key, size in (
        ("src", edges), ("tlo", edges), ("thi", edges), ("rel", edges), ("lab", edges), ("nlo", negs), ("nhi", negs),
    ):
        starts[key] = (at, size)
        at += size
    return starts, at


def task_rows(edges, negs, width):
    total = field_starts(edges, negs)[1]
    return -(-total // width // 8) * 8 if total % width == 0 else (-(-(-(-total // width)) // 8)) * 8


def pack(fields, rows, src, tgt, rel, neg, lab, flat):
    slots = src.shape[2]
    width = flat.shape[1]
    flat[...] = jnp.zeros_like(flat)
    for m in range(slots):
        tgt_f = tgt[0, 0, m : m + 1, :].astype(F32)
        neg_f = neg[0, 0, m : m + 1, :].astype(F32)
        t_hi = jnp.floor(tgt_f * (1.0 / 256))
        n_hi = jnp.floor(neg_f * (1.0 / 256))
        values = {
            "src": src[0, 0, m : m + 1, :].astype(F32), "tlo": tgt_f - 256.0 * t_hi, "thi": t_hi,
            "rel": rel[m : m + 1, :].astype(F32), "lab": lab[0, 0, m : m + 1, :].astype(F32),
            "nlo": neg_f - 256.0 * n_hi, "nhi": n_hi,
        }
        for key, (at, size) in fields.items():
            done = 0
            while done < size:
                row, col = divmod(at + done, width)
                n = min(width - col, size - done)
                flat[m * rows + row : m * rows + row + 1, col : col + n] = values[key][:, done : done + n]
                done += n


def first_body(fields, rows, src_feat, tgt_feat, weight, src, tgt, rel, neg, lab, shift, out, act, feats, flat):
    pack(fields, rows, src, tgt, rel, neg, lab, flat)
    n = src_feat.shape[0]
    value = jnp.tanh(dot(src_feat[...], weight[...], NN))
    act[...] = value
    out[:n, :] = value.astype(BF16)
    tasks = flat.shape[0]
    out[n : n + tasks, :] = flat[...].astype(BF16)
    out[n + tasks :, :] = jnp.zeros_like(out[n + tasks :, :])
    out[n + tasks : n + tasks + shift.shape[0], :] = shift[...]
    feats[:n, :] = src_feat[...]
    feats[n:, :] = tgt_feat[...]


def take(block, fields, key):
    at, size = fields[key]
    width = block.shape[1]
    pieces, done = [], 0
    while done < size:
        row, col = divmod(at + done, width)
        n = min(width - col, size - done)
        pieces.append(block[row : row + 1, col : col + n])
        done += n
    return pieces[0] if len(pieces) == 1 else jnp.concatenate(pieces, axis=1)


def wrapped(value, base, count):
    moved = value - base
    return jnp.where(moved < 0, moved + count, moved)


def one_hot(rows, ids, value=None):
    one = jnp.full(ids.shape, 1.0, BF16) if value is None else value.astype(BF16)
    pieces = []
    for base in range(0, rows, 256):
        n = min(256, rows - base)
        local = jnp.where((ids >= base) & (ids < base + n), ids - base, -1.0).astype(BF16)
        iota = lax.broadcasted_iota(jnp.int32, (n, ids.shape[1]), 0).astype(F32).astype(BF16)
        pieces.append(jnp.where(iota == local, one, jnp.zeros_like(one)))
    return pieces[0] if len(pieces) == 1 else jnp.concatenate(pieces, axis=0)


def own_quarter(size):
    me = lax.axis_index("bucket")
    return (me & 1) * 2 + ((me >> (size.bit_length() - 2)) & 1)


def own_half():
    return (lax.axis_index("bucket") >> 1) & 1


def aligned(number, size, base=0):
    return pl.ds(pl.multiple_of(base + number * size, size), size)


def prepare_body(size, s_rows, own, low, high, far, weight, emb, act, turned, held):
    t_rows = own.shape[0] - s_rows
    me = own_quarter(size)
    for j, x in enumerate((own, low, high, far)):
        held[aligned(me ^ APART[j], s_rows), :] = x[:s_rows, :]
        held[pl.ds(pl.multiple_of(4 * s_rows + (me ^ APART[j]) * t_rows, s_rows), t_rows), :] = x[s_rows:, :]
        emb[j * t_rows : (j + 1) * t_rows, :] = jnp.tanh(dot(x[s_rows:, :], weight[...], NN)).astype(BF16)
    columns = weight[:, aligned(me, act.shape[1])]
    act[...] = jnp.tanh(dot(held[4 * s_rows :, :], columns, NN))
    turned[...] = held[...].astype(F32).T.astype(BF16)


def start_all(copies, sems):
    started = [pltpu.make_async_copy(a, b, sems.at[i]) for i, (a, b) in enumerate(copies)]
    for c in started:
        c.start()
    for c in started:
        c.wait()


def spread(pieces, targets):
    own, plus, minus, far_a, far_b = pieces
    copies = []
    half = far_a.shape[0]
    for place, parts in ((0, ((own, 0),)), (1, ((plus, 0),)), (2, ((far_a, 0), (far_b, half))), (3, ((minus, 0),))):
        for lo, hi, ref in targets(place):
            for part, base in parts:
                a, b = max(lo, base), min(hi, base + part.shape[0])
                if a < b:
                    copies.append((part.at[pl.ds(a - base, b - a)], ref.at[pl.ds(a - lo, b - a)]))
    return copies


def weights_of(scores, coded, pairs, scale):
    sig = 1.0 / (1.0 + jnp.exp2(scores * (-scale * LOG2E)))
    labels = jnp.floor(coded * (1.0 / LABELLED))
    edges = coded - (LABELLED - 1.0) * labels
    return edges * sig - labels + pairs * sig.astype(BF16).astype(F32)


def meets_body(cfg, own, plus, minus, far_a, far_b, tgt, *refs):
    fields, rows, s_rows, t_rows, n_rel, scale, groups, negs, size = cfg
    t_outs, s_keep, s_send = refs[:4], refs[4], refs[5]
    src, idx, query, parts, acc, w_src, w_rel, total, sems = refs[6:]
    ring = lax.axis_index("rel")
    tasks = idx.shape[1] - 16

    def places(place):
        return (0, s_rows, src.at[pl.ds(place * s_rows, s_rows)]), (s_rows, own.shape[0], idx.at[place])

    start_all(spread((own, plus, minus, far_a, far_b), places), sems)
    for ref in (acc, w_src, w_rel):
        ref[...] = jnp.zeros_like(ref)
    all_src = src.shape[0]
    all_tgt = t_rows * groups
    src_base = (ring * s_rows).astype(F32)
    tgt_base = (ring * t_rows).astype(F32)
    lane = lax.broadcasted_iota(jnp.int32, (t_rows, w_rel.shape[1]), 1)

    def step(group, carry):
        shift = idx[group, tasks : tasks + 16, :]
        place = lax.rem(group + ring, groups) * n_rel
        for k in range(n_rel):
            query[k * all_src : (k + 1) * all_src, :] = src[...] + shift[k : k + 1, :]
        scores = dot(tgt[...], query[...], NT)
        for j, slot in enumerate(SLOT_OF):
            block = idx[group, slot * rows : (slot + 1) * rows, :].astype(F32)
            who = wrapped(take(block, fields, "src"), src_base, float(all_src))
            rel = take(block, fields, "rel")
            ids = wrapped(take(block, fields, "thi") * 256.0 + take(block, fields, "tlo"), tgt_base, float(all_tgt))
            weight = 1.0 + (LABELLED - 1.0) * take(block, fields, "lab")
            left = [one_hot(t_rows, jnp.where(rel == float(k), ids, -1.0), weight) for k in range(n_rel)]
            left.append(one_hot(16, rel))
            counts = dot(jnp.concatenate(left, axis=0), one_hot(all_src, who), NT)
            neg = wrapped(take(block, fields, "nhi") * 256.0 + take(block, fields, "nlo"), tgt_base, float(all_tgt))
            neg_count = jnp.sum(one_hot(t_rows, neg).astype(F32), axis=1, keepdims=True) * (1.0 / negs)
            mine = slice(j * t_rows, (j + 1) * t_rows)
            part, line = None, jnp.zeros((t_rows, w_rel.shape[1]), F32)
            for k in range(n_rel):
                top = k * t_rows
                each = n_rel * t_rows + k
                lanes = slice(k * all_src, (k + 1) * all_src)
                value = weights_of(
                    scores[mine, lanes], counts[top : top + t_rows, :], neg_count * counts[each : each + 1, :], scale
                )
                high = value.astype(BF16)
                parts[2 * j * t_rows : (2 * j + 1) * t_rows, lanes] = high
                parts[(2 * j + 1) * t_rows : (2 * j + 2) * t_rows, lanes] = (value - high.astype(F32)).astype(BF16)
                part = value if part is None else part + value
                line = jnp.where(lane == place + k, jnp.sum(value, axis=1, keepdims=True), line)
            w_src[mine, :] += part
            w_rel[mine, :] += line
        acc[...] += dot(parts[...], query[...], NN)
        return carry

    lax.fori_loop(0, groups, step, 0)
    whole = jnp.concatenate([w_src[...].T, w_rel[...].T[:16, :]], axis=0)
    high = whole.astype(BF16)
    low = (whole - high.astype(F32)).astype(BF16)
    total[...] = scale * (dot(high, tgt[...], NN) + dot(low, tgt[...], NN))
    for r in range(groups):
        out = s_send if r % 2 else s_keep
        place = lax.rem((ring ^ r) - ring + groups, groups)
        out[(r // 2) * s_rows : (r // 2 + 1) * s_rows, :] = total[aligned(place, s_rows), :]
    me = own_quarter(size)
    for i, out in enumerate(t_outs):
        lanes = aligned(me ^ APART[i], out.shape[1])
        for j in range(4):
            high, low = acc[2 * j * t_rows : (2 * j + 1) * t_rows, lanes], acc[(2 * j + 1) * t_rows : (2 * j + 2) * t_rows, lanes]
            out[aligned(me ^ APART[j], t_rows), :] = scale * (high + low)
        out[4 * t_rows :, :] = total[all_src:, lanes]


def source_body(size, keep, recv, last, act, grad, *outs):
    n = grad.shape[0]
    value = (keep[:n, :] + recv[:n, :]) + last[...]
    grad[...] = value
    d = (value * (1.0 - act[...] * act[...])).astype(BF16)
    wide = outs[0].shape[1]
    me = own_quarter(size)
    for a in range(4):
        for j, out in enumerate(outs):

            @pl.when((me ^ APART[j]) == a)
            def _():
                out[...] = d[:, a * wide : (a + 1) * wide]


def target_body(size, keep, recv, last, act, turned, *outs):
    parts, rows = outs[:2], outs[2:]
    value = (keep[...] + recv[...]) + last[...]
    n = act.shape[0]
    d = (value[:n, :] * (1.0 - act[...] * act[...])).astype(BF16)
    block = turned.shape[0] // 2
    first = turned.shape[1] - n
    for r, out in enumerate(parts):
        out[:block, :] = dot(turned[aligned(own_half() ^ r, block), first:], d, NN)
        out[block:, :] = value[n:, :]
    me = own_quarter(size)
    for a in range(4):
        for j, out in enumerate(rows):

            @pl.when((me ^ APART[j]) == a)
            def _():
                out[...] = value[a * (n // 4) : (a + 1) * (n // 4), :]


def join_body(size, keep_in, send_in, turned, *refs):
    pieces, (keep, send), held = refs[:4], refs[4:6], refs[6]
    n = pieces[0].shape[0]
    me = own_quarter(size)
    for j, x in enumerate(pieces):
        held[aligned(me ^ APART[j], n), :] = x[...]
    block = turned.shape[0] // 2
    for r, (x, out) in enumerate(((keep_in, keep), (send_in, send))):
        out[:block, :] = x[:block, :] + dot(turned[aligned(own_half() ^ r, block), : 4 * n], held[...], NN)
        out[block:, :] = x[block:, :]


def rows_body(size, *refs):
    parts, (grad,) = refs[:4], refs[4:]
    me = own_quarter(size)
    for j, x in enumerate(parts):
        grad[:, aligned(me ^ APART[j], x.shape[1])] = x[...]


def place_body(size, *refs):
    blocks, (enc_grad, rel_grad) = refs[:8], refs[8:]
    block = enc_grad.shape[0] // 2
    me = own_quarter(size)
    n_rel = rel_grad.shape[0]
    for r in range(2):
        for j in range(4):
            x = blocks[r * 4 + j]
            lanes = aligned(me ^ APART[j], x.shape[1])
            enc_grad[aligned(own_half() ^ r, block), lanes] = x[:block, :]
            if r == 0:
                for k in range(n_rel):
                    rel_grad[k : k + 1, lanes] = x[pl.ds(block + lax.axis_index("rel") * n_rel + k, 1), :]


def shards(src_feat, tgt_feat, enc_weight, rel_shift, edge_src, edge_tgt, rel_hot, neg_idx, edge_label):
    buckets = lax.axis_size("bucket")
    groups = lax.axis_size("rel")
    half = buckets // 2
    s_rows, t_rows = src_feat.shape[0], tgt_feat.shape[0]
    feat, emb = enc_weight.shape
    slots, edges = edge_src.shape[2:]
    negs = neg_idx.shape[3]
    n_rel = rel_hot.shape[3]
    fields, _ = field_starts(edges, negs)
    rows = task_rows(edges, negs, emb)
    cfg = (fields, rows, s_rows, t_rows, n_rel, emb**-0.5, groups, negs, buckets)
    n = s_rows + t_rows
    wide = emb // 4

    def met(x, mask):
        return lax.ppermute(x, "bucket", [(i, i ^ mask) for i in range(buckets)])

    def ring(x, step):
        return lax.ppermute(x, "rel", [(i, (i - step) % groups) for i in range(groups)])

    def crossed(x, mask):
        return lax.ppermute(x, "rel", [(i, i ^ mask) for i in range(groups)])

    def around(x):
        cut_at = x.shape[0] // 2
        plus, minus = ring(x, 1), ring(x, -1)
        return x, plus, minus, ring(plus[:cut_at], 1), ring(minus[cut_at:], -1)

    def shared(parts):
        return [parts[0], met(parts[1], 1), met(parts[2], half), met(parts[3], half + 1)]

    which = sum(k * rel_hot[0, 0, :, k, :] for k in range(1, n_rel))
    own, s_act, feats = call(
        functools.partial(first_body, fields, rows),
        [shaped((s_rows + slots * rows + 16, emb), BF16), shaped((s_rows, emb)), shaped((n, feat), BF16)],
        [src_feat, tgt_feat, enc_weight, edge_src, edge_tgt, which, neg_idx, edge_label, rel_shift],
        scratch=[pltpu.VMEM((slots * rows, emb), F32)],
        flops=2 * s_rows * feat * emb,
    )
    first = around(own)
    f_high = met(feats, half)
    f_low = met(feats, 1)
    f_far = met(f_high, 1)
    tgt, act, turned = call(
        functools.partial(prepare_body, buckets, s_rows),
        [shaped((4 * t_rows, emb), BF16), shaped((4 * t_rows, wide)), shaped((feat, 4 * n), BF16)],
        [feats, f_low, f_high, f_far, enc_weight],
        scratch=[pltpu.VMEM((4 * n, feat), BF16)],
        flops=8 * n * feat * emb,
    )
    queries = n_rel * groups * s_rows
    *t_parts, s_keep, s_send = call(
        functools.partial(meets_body, cfg),
        [shaped((4 * t_rows + 16, wide))] * 4 + [shaped((groups // 2 * s_rows, emb))] * 2,
        [*first, tgt],
        in_specs=[ANY] * 5 + [VMEM],
        scratch=[
            pltpu.VMEM((groups * s_rows, emb), BF16),
            pltpu.VMEM((groups, slots * rows + 16, emb), BF16),
            pltpu.VMEM((queries, emb), BF16),
            pltpu.VMEM((8 * t_rows, queries), BF16),
            pltpu.VMEM((8 * t_rows, emb), F32),
            pltpu.VMEM((4 * t_rows, groups * s_rows), F32),
            pltpu.VMEM((4 * t_rows, 128), F32),
            pltpu.VMEM((groups * s_rows + 16, emb), F32),
            pltpu.SemaphoreType.DMA((32,)),
        ],
        flops=12e9,
    )
    s_recv = crossed(s_send, 1)
    t_recv, t_next = met(t_parts[1], 1), met(t_parts[3], 1)
    t_last = met(t_parts[2] + t_next, half)
    s_last = crossed(s_keep[s_rows:] + s_recv[s_rows:], 2)
    part = feat // 2
    keep, send, *g_parts = call(
        functools.partial(target_body, buckets),
        [shaped((part + 16, wide))] * 2 + [shaped((t_rows, wide))] * 4,
        [t_parts[0], t_recv, t_last, act, turned],
        flops=8 * t_rows * feat * wide,
    )
    keep, send, s_last = lax.optimization_barrier((keep, send, s_last))
    src_grad, *d_parts = call(
        functools.partial(source_body, buckets),
        [shaped((s_rows, emb))] + [shaped((s_rows, wide), BF16)] * 4,
        [s_keep, s_recv, s_last, s_act],
    )
    keep, send = call(
        functools.partial(join_body, buckets),
        [shaped((part + 16, wide))] * 2,
        [keep, send, turned, *shared(d_parts)],
        scratch=[pltpu.VMEM((4 * s_rows, wide), BF16)],
        flops=8 * s_rows * feat * wide,
    )
    got = met(send, 2)
    g_parts, got = lax.optimization_barrier((shared(g_parts), got))
    joint = keep + got
    (tgt_grad,) = call(functools.partial(rows_body, buckets), [shaped((t_rows, emb))], g_parts)
    for bit in range(2, buckets.bit_length() - 2):
        joint = joint + met(joint, 1 << bit)
    got = crossed(joint, 1)
    tgt_grad, got = lax.optimization_barrier((tgt_grad, got))
    joint = joint + got
    joint = joint + crossed(joint, 3)
    same = [joint, met(joint, half), met(joint, 2), met(joint, half + 2)]
    other = [met(x, 1) for x in same]
    blocks = [same[0], other[0], same[1], other[1], same[2], other[2], same[3], other[3]]
    enc_grad, rel_grad = call(
        functools.partial(place_body, buckets), [shaped((feat, emb)), shaped((n_rel, emb))], blocks
    )
    return (src_grad, tgt_grad, rel_grad, enc_grad)


def solution(mesh):
    in_specs = (
        P(("bucket", "rel"), None),
        P(("bucket", "rel"), None),
        P(),
        P("rel", None),
        P("bucket", "rel", None, None),
        P("bucket", "rel", None, None),
        P("bucket", "rel", None, None, None),
        P("bucket", "rel", None, None),
        P("bucket", "rel", None, None),
    )
    out_specs = (P(("bucket", "rel"), None), P(("bucket", "rel"), None), P("rel", None), P())

    return jax.shard_map(shards, mesh=mesh, in_specs=in_specs, out_specs=out_specs, check_vma=False)
```

```python
import functools

import jax
import jax.numpy as jnp
from jax import lax
from jax.experimental import pallas as pl
from jax.experimental.pallas import tpu as pltpu
from jax.sharding import PartitionSpec as P


CHUNKS = 2
LABELLED = 1024.0
LOG2E = 1.4426950408889634
SLOT_OF = (0, 1, 3, 2)
APART = (0, 2, 1, 3)
NT = (((1,), (1,)), ((), ()))
NN = (((1,), (0,)), ((), ()))
F32 = jnp.float32
BF16 = jnp.bfloat16
VMEM = pl.BlockSpec(memory_space=pltpu.VMEM)
ANY = pl.BlockSpec(memory_space=pl.ANY)


def dot(a, b, dims):
    return lax.dot_general(a, b, dims, preferred_element_type=F32)


def call(body, outs, ins, in_specs=None, scratch=(), flops=0):
    moved = sum(x.size * x.dtype.itemsize for x in ins)
    moved += sum(o.size * o.dtype.itemsize for o in outs)
    return pl.pallas_call(
        body,
        out_shape=tuple(outs),
        in_specs=in_specs or [VMEM] * len(ins),
        out_specs=tuple(VMEM for _ in outs),
        scratch_shapes=scratch,
        cost_estimate=pl.CostEstimate(flops=int(flops), bytes_accessed=int(moved), transcendentals=0),
    )(*ins)


def shaped(shape, dtype=F32):
    return jax.ShapeDtypeStruct(tuple(shape), dtype)


def field_starts(edges, negs):
    starts, at = {}, 0
    for key, size in (
        ("src", edges), ("tlo", edges), ("thi", edges), ("rel", edges), ("lab", edges), ("nlo", negs), ("nhi", negs),
    ):
        starts[key] = (at, size)
        at += size
    return starts, at


def task_rows(edges, negs, width):
    total = field_starts(edges, negs)[1]
    return -(-total // width // 8) * 8 if total % width == 0 else (-(-(-(-total // width)) // 8)) * 8


def pack(fields, rows, src, tgt, rel, neg, lab, flat):
    slots = src.shape[2]
    width = flat.shape[1]
    flat[...] = jnp.zeros_like(flat)
    for m in range(slots):
        tgt_f = tgt[0, 0, m : m + 1, :].astype(F32)
        neg_f = neg[0, 0, m : m + 1, :].astype(F32)
        t_hi = jnp.floor(tgt_f * (1.0 / 256))
        n_hi = jnp.floor(neg_f * (1.0 / 256))
        values = {
            "src": src[0, 0, m : m + 1, :].astype(F32), "tlo": tgt_f - 256.0 * t_hi, "thi": t_hi,
            "rel": rel[m : m + 1, :].astype(F32), "lab": lab[0, 0, m : m + 1, :].astype(F32),
            "nlo": neg_f - 256.0 * n_hi, "nhi": n_hi,
        }
        for key, (at, size) in fields.items():
            done = 0
            while done < size:
                row, col = divmod(at + done, width)
                n = min(width - col, size - done)
                flat[m * rows + row : m * rows + row + 1, col : col + n] = values[key][:, done : done + n]
                done += n


def first_body(fields, rows, src_feat, weight, src, tgt, rel, neg, lab, shift, out, act, flat):
    pack(fields, rows, src, tgt, rel, neg, lab, flat)
    n = src_feat.shape[0]
    value = jnp.tanh(dot(src_feat[...], weight[...], NN))
    act[...] = value
    out[:n, :] = value.astype(BF16)
    tasks = flat.shape[0]
    out[n : n + tasks, :] = flat[...].astype(BF16)
    out[n + tasks :, :] = jnp.zeros_like(out[n + tasks :, :])
    out[n + tasks : n + tasks + shift.shape[0], :] = shift[...]


def take(block, fields, key):
    at, size = fields[key]
    width = block.shape[1]
    pieces, done = [], 0
    while done < size:
        row, col = divmod(at + done, width)
        n = min(width - col, size - done)
        pieces.append(block[row : row + 1, col : col + n])
        done += n
    return pieces[0] if len(pieces) == 1 else jnp.concatenate(pieces, axis=1)


def wrapped(value, base, count):
    moved = value - base
    return jnp.where(moved < 0, moved + count, moved)


def one_hot(rows, ids, value=None):
    one = jnp.full(ids.shape, 1.0, BF16) if value is None else value.astype(BF16)
    pieces = []
    for base in range(0, rows, 256):
        n = min(256, rows - base)
        local = jnp.where((ids >= base) & (ids < base + n), ids - base, -1.0).astype(BF16)
        iota = lax.broadcasted_iota(jnp.int32, (n, ids.shape[1]), 0).astype(F32).astype(BF16)
        pieces.append(jnp.where(iota == local, one, jnp.zeros_like(one)))
    return pieces[0] if len(pieces) == 1 else jnp.concatenate(pieces, axis=0)


def own_quarter(size):
    me = lax.axis_index("bucket")
    return (me & 1) * 2 + ((me >> (size.bit_length() - 2)) & 1)


def own_half():
    return (lax.axis_index("bucket") >> 1) & 1


def aligned(number, size, base=0):
    return pl.ds(pl.multiple_of(base + number * size, size), size)


def encode_body(own, low, high, far, weight, emb, held):
    n = own.shape[0]
    for j, x in enumerate((own, low, high, far)):
        held[j * n : (j + 1) * n, :] = x[...]
    emb[...] = jnp.tanh(dot(held[...], weight[...], NN)).astype(BF16)


def prepare_body(size, *refs):
    src, tgt, weight, (act, src_turned, tgt_turned, src_held, tgt_held) = refs[:4], refs[4:8], refs[8], refs[9:]
    me = own_quarter(size)
    for feats, held, turned in ((src, src_held, src_turned), (tgt, tgt_held, tgt_turned)):
        for j, x in enumerate(feats):
            held[aligned(me ^ APART[j], x.shape[0]), :] = x[...]
        turned[...] = held[...].astype(F32).T.astype(BF16)
    act[...] = jnp.tanh(dot(tgt_held[...], weight[:, aligned(me, act.shape[1])], NN))


def start_all(copies, sems):
    started = [pltpu.make_async_copy(a, b, sems.at[i]) for i, (a, b) in enumerate(copies)]
    for c in started:
        c.start()
    for c in started:
        c.wait()


def spread(pieces, targets):
    own, plus, minus, far_a, far_b = pieces
    copies = []
    half = far_a.shape[0]
    for place, parts in ((0, ((own, 0),)), (1, ((plus, 0),)), (2, ((far_a, 0), (far_b, half))), (3, ((minus, 0),))):
        for lo, hi, ref in targets(place):
            for part, base in parts:
                a, b = max(lo, base), min(hi, base + part.shape[0])
                if a < b:
                    copies.append((part.at[pl.ds(a - base, b - a)], ref.at[pl.ds(a - lo, b - a)]))
    return copies


def weights_of(scores, coded, pairs, scale):
    sig = 1.0 / (1.0 + jnp.exp2(scores * (-scale * LOG2E)))
    labels = jnp.floor(coded * (1.0 / LABELLED))
    edges = coded - (LABELLED - 1.0) * labels
    return edges * sig - labels + pairs * sig.astype(BF16).astype(F32)


def meets_body(cfg, own, plus, minus, far_a, far_b, tgt, *refs):
    fields, rows, s_rows, t_rows, n_rel, scale, groups, negs, size = cfg
    t_outs, s_outs = refs[:4], refs[4:8]
    src, idx, query_a, query_b, parts_a, parts_b, acc, w_src, w_rel, total, sems = refs[8:]
    ring = lax.axis_index("rel")
    tasks = idx.shape[1] - 16

    def places(place):
        return (0, s_rows, src.at[pl.ds(place * s_rows, s_rows)]), (s_rows, own.shape[0], idx.at[place])

    start_all(spread((own, plus, minus, far_a, far_b), places), sems)
    for ref in (acc, w_src, w_rel, query_b, parts_b):
        ref[...] = jnp.zeros_like(ref)
    all_src = src.shape[0]
    all_tgt = t_rows * groups
    src_base = (ring * s_rows).astype(F32)
    tgt_base = (ring * t_rows).astype(F32)
    lane = lax.broadcasted_iota(jnp.int32, (t_rows, w_rel.shape[1]), 1)

    def one_group(group, query, parts):
        shift = idx[group, tasks : tasks + 16, :]
        place = lax.rem(group + ring, groups) * n_rel
        for k in range(n_rel):
            query[k * all_src : (k + 1) * all_src, :] = src[...] + shift[k : k + 1, :]
        scores = dot(tgt[...], query[...], NT)
        for j, slot in enumerate(SLOT_OF):
            block = idx[group, slot * rows : (slot + 1) * rows, :].astype(F32)
            who = wrapped(take(block, fields, "src"), src_base, float(all_src))
            rel = take(block, fields, "rel")
            ids = wrapped(take(block, fields, "thi") * 256.0 + take(block, fields, "tlo"), tgt_base, float(all_tgt))
            weight = 1.0 + (LABELLED - 1.0) * take(block, fields, "lab")
            left = [one_hot(t_rows, jnp.where(rel == float(k), ids, -1.0), weight) for k in range(n_rel)]
            left.append(one_hot(16, rel))
            counts = dot(jnp.concatenate(left, axis=0), one_hot(all_src, who), NT)
            neg = wrapped(take(block, fields, "nhi") * 256.0 + take(block, fields, "nlo"), tgt_base, float(all_tgt))
            neg_count = jnp.sum(one_hot(t_rows, neg).astype(F32), axis=1, keepdims=True) * (1.0 / negs)
            mine = slice(j * t_rows, (j + 1) * t_rows)
            part, line = None, jnp.zeros((t_rows, w_rel.shape[1]), F32)
            for k in range(n_rel):
                top = k * t_rows
                each = n_rel * t_rows + k
                lanes = slice(k * all_src, (k + 1) * all_src)
                value = weights_of(
                    scores[mine, lanes], counts[top : top + t_rows, :], neg_count * counts[each : each + 1, :], scale
                )
                high = value.astype(BF16)
                parts[2 * j * t_rows : (2 * j + 1) * t_rows, lanes] = high
                parts[(2 * j + 1) * t_rows : (2 * j + 2) * t_rows, lanes] = (value - high.astype(F32)).astype(BF16)
                part = value if part is None else part + value
                line = jnp.where(lane == place + k, jnp.sum(value, axis=1, keepdims=True), line)
            w_src[mine, :] += part
            w_rel[mine, :] += line

    def step(pair, carry):
        one_group(2 * pair, query_a, parts_a)
        acc[...] += dot(parts_b[...], query_b[...], NN)
        one_group(2 * pair + 1, query_b, parts_b)
        acc[...] += dot(parts_a[...], query_a[...], NN)
        return carry

    lax.fori_loop(0, groups // 2, step, 0)
    acc[...] += dot(parts_b[...], query_b[...], NN)
    whole = jnp.concatenate([w_src[...].T, w_rel[...].T[:16, :]], axis=0)
    high = whole.astype(BF16)
    low = (whole - high.astype(F32)).astype(BF16)
    total[...] = scale * (dot(high, tgt[...], NN) + dot(low, tgt[...], NN))
    for r, out in enumerate(s_outs):
        place = lax.rem((ring ^ r) - ring + groups, groups)
        out[...] = total[aligned(place, s_rows), :]
    me = own_quarter(size)
    for i, out in enumerate(t_outs):
        lanes = aligned(me ^ APART[i], out.shape[1])
        for j in range(4):
            high, low = acc[2 * j * t_rows : (2 * j + 1) * t_rows, lanes], acc[(2 * j + 1) * t_rows : (2 * j + 2) * t_rows, lanes]
            out[aligned(me ^ APART[j], t_rows), :] = scale * (high + low)
        out[4 * t_rows :, :] = total[all_src:, lanes]


def source_body(size, a, b, c, d, act, grad, *outs):
    value = (a[...] + b[...]) + (c[...] + d[...])
    grad[...] = value
    d = (value * (1.0 - act[...] * act[...])).astype(BF16)
    wide = outs[0].shape[1]
    me = own_quarter(size)
    for a in range(4):
        for j, out in enumerate(outs):

            @pl.when((me ^ APART[j]) == a)
            def _():
                out[...] = d[:, a * wide : (a + 1) * wide]


def target_body(size, keep, recv, last, act, turned, *outs):
    parts, rows = outs[:2], outs[2:]
    value = (keep[...] + recv[...]) + last[...]
    n = act.shape[0]
    d = (value[:n, :] * (1.0 - act[...] * act[...])).astype(BF16)
    block = turned.shape[0] // 2
    for r, out in enumerate(parts):
        out[:block, :] = dot(turned[aligned(own_half() ^ r, block), :], d, NN)
        out[block:, :] = value[n:, :]
    me = own_quarter(size)
    for a in range(4):
        for j, out in enumerate(rows):

            @pl.when((me ^ APART[j]) == a)
            def _():
                out[...] = value[a * (n // 4) : (a + 1) * (n // 4), :]


def join_body(size, keep_in, send_in, turned, *refs):
    pieces, outs, held = refs[:4], refs[4:-1], refs[-1]
    n = pieces[0].shape[0]
    me = own_quarter(size)
    for j, x in enumerate(pieces):
        held[aligned(me ^ APART[j], n), :] = x[...]
    block = turned.shape[0] // 2
    part = block // CHUNKS
    for r, x in enumerate((keep_in, send_in)):
        added = dot(turned[aligned(own_half() ^ r, block), :], held[...], NN)
        for c, out in enumerate(outs[r * CHUNKS : (r + 1) * CHUNKS]):
            out[:part, :] = x[c * part : (c + 1) * part, :] + added[c * part : (c + 1) * part, :]
            if c == 0:
                out[part:, :] = x[block:, :]


def rows_body(size, *refs):
    parts, (grad,) = refs[:4], refs[4:]
    me = own_quarter(size)
    for j, x in enumerate(parts):
        grad[:, aligned(me ^ APART[j], x.shape[1])] = x[...]


def place_body(size, *refs):
    blocks, (enc_grad, rel_grad) = refs[:-2], refs[-2:]
    part = enc_grad.shape[0] // 2 // CHUNKS
    me = own_quarter(size)
    n_rel = rel_grad.shape[0]
    for at, x in enumerate(blocks):
        r, c, j = at // (4 * CHUNKS), at // 4 % CHUNKS, at % 4
        lanes = aligned(me ^ APART[j], x.shape[1])
        enc_grad[aligned((own_half() ^ r) * CHUNKS + c, part), lanes] = x[:part, :]
        if r == 0 and c == 0:
            for k in range(n_rel):
                rel_grad[k : k + 1, lanes] = x[pl.ds(part + lax.axis_index("rel") * n_rel + k, 1), :]


def shards(src_feat, tgt_feat, enc_weight, rel_shift, edge_src, edge_tgt, rel_hot, neg_idx, edge_label):
    buckets = lax.axis_size("bucket")
    groups = lax.axis_size("rel")
    half = buckets // 2
    s_rows, t_rows = src_feat.shape[0], tgt_feat.shape[0]
    feat, emb = enc_weight.shape
    slots, edges = edge_src.shape[2:]
    negs = neg_idx.shape[3]
    n_rel = rel_hot.shape[3]
    fields, _ = field_starts(edges, negs)
    rows = task_rows(edges, negs, emb)
    cfg = (fields, rows, s_rows, t_rows, n_rel, emb**-0.5, groups, negs, buckets)
    wide = emb // 4

    def met(x, mask):
        return lax.ppermute(x, "bucket", [(i, i ^ mask) for i in range(buckets)])

    def ring(x, step):
        return lax.ppermute(x, "rel", [(i, (i - step) % groups) for i in range(groups)])

    def crossed(x, mask):
        return lax.ppermute(x, "rel", [(i, i ^ mask) for i in range(groups)])

    def around(x):
        cut_at = x.shape[0] // 2
        plus, minus = ring(x, 1), ring(x, -1)
        return x, plus, minus, ring(plus[:cut_at], 1), ring(minus[cut_at:], -1)

    def shared(parts):
        return [parts[0], met(parts[1], 1), met(parts[2], half), met(parts[3], half + 1)]

    which = sum(k * rel_hot[0, 0, :, k, :] for k in range(1, n_rel))
    own, s_act = call(
        functools.partial(first_body, fields, rows),
        [shaped((s_rows + slots * rows + 16, emb), BF16), shaped((s_rows, emb))],
        [src_feat, enc_weight, edge_src, edge_tgt, which, neg_idx, edge_label, rel_shift],
        scratch=[pltpu.VMEM((slots * rows, emb), F32)],
        flops=2 * s_rows * feat * emb,
    )
    first = around(own)

    def fetched(x):
        high = met(x, half)
        return [x, met(x, 1), high, met(high, 1)]

    t_feats, s_feats = fetched(tgt_feat), fetched(src_feat)
    (tgt,) = call(
        encode_body,
        [shaped((4 * t_rows, emb), BF16)],
        [*t_feats, enc_weight],
        scratch=[pltpu.VMEM((4 * t_rows, feat), BF16)],
        flops=8 * t_rows * feat * emb,
    )
    queries = n_rel * groups * s_rows
    tgt, s_feats = lax.optimization_barrier((tgt, s_feats))
    parts = call(
        functools.partial(meets_body, cfg),
        [shaped((4 * t_rows + 16, wide))] * 4 + [shaped((s_rows, emb))] * groups,
        [*first, tgt],
        in_specs=[ANY] * 5 + [VMEM],
        scratch=[
            pltpu.VMEM((groups * s_rows, emb), BF16),
            pltpu.VMEM((groups, slots * rows + 16, emb), BF16),
            pltpu.VMEM((queries, emb), BF16),
            pltpu.VMEM((queries, emb), BF16),
            pltpu.VMEM((8 * t_rows, queries), BF16),
            pltpu.VMEM((8 * t_rows, queries), BF16),
            pltpu.VMEM((8 * t_rows, emb), F32),
            pltpu.VMEM((4 * t_rows, groups * s_rows), F32),
            pltpu.VMEM((4 * t_rows, 128), F32),
            pltpu.VMEM((groups * s_rows + 16, emb), F32),
            pltpu.SemaphoreType.DMA((32,)),
        ],
        flops=12e9,
    )
    t_parts, s_parts = parts[:4], parts[4:]
    s_parts = [s_parts[0], *(crossed(s_parts[mask], mask) for mask in range(1, groups))]
    t_recv, t_next = met(t_parts[1], 1), met(t_parts[3], 1)
    t_last = met(t_parts[2] + t_next, half)
    s_feats, t_recv = lax.optimization_barrier((s_feats, t_recv))
    act, s_turned, t_turned = call(
        functools.partial(prepare_body, buckets),
        [shaped((4 * t_rows, wide)), shaped((feat, 4 * s_rows), BF16), shaped((feat, 4 * t_rows), BF16)],
        [*s_feats, *t_feats, enc_weight],
        scratch=[pltpu.VMEM((4 * s_rows, feat), BF16), pltpu.VMEM((4 * t_rows, feat), BF16)],
        flops=8 * t_rows * feat * wide,
    )
    s_parts, act = lax.optimization_barrier((s_parts, act))
    part = feat // 2
    src_grad, *d_parts = call(
        functools.partial(source_body, buckets),
        [shaped((s_rows, emb))] + [shaped((s_rows, wide), BF16)] * 4,
        [*s_parts, s_act],
    )
    d_parts, t_last = lax.optimization_barrier((d_parts, t_last))
    keep, send, *g_parts = call(
        functools.partial(target_body, buckets),
        [shaped((part + 16, wide))] * 2 + [shaped((t_rows, wide))] * 4,
        [t_parts[0], t_recv, t_last, act, t_turned],
        flops=8 * t_rows * feat * wide,
    )
    d_parts = shared(d_parts)
    piece = part // CHUNKS
    sizes = [shaped((piece + (16 if c == 0 else 0), wide)) for c in range(CHUNKS)] * 2
    halves = call(
        functools.partial(join_body, buckets),
        sizes,
        [keep, send, s_turned, *d_parts],
        scratch=[pltpu.VMEM((4 * s_rows, wide), BF16)],
        flops=8 * s_rows * feat * wide,
    )
    got = [met(x, 2) for x in halves[CHUNKS:]]
    g_parts, got[0] = lax.optimization_barrier((shared(g_parts), got[0]))
    (tgt_grad,) = call(functools.partial(rows_body, buckets), [shaped((t_rows, emb))], g_parts)
    blocks = [[], []]
    for c in range(CHUNKS):
        joint = halves[c] + got[c]
        for bit in range(2, buckets.bit_length() - 2):
            joint = joint + met(joint, 1 << bit)
        joint = joint + crossed(joint, 1)
        if c == 0:
            tgt_grad, joint = lax.optimization_barrier((tgt_grad, joint))
        joint = joint + crossed(joint, 3)
        for r, same in ((0, [joint, met(joint, half)]), (1, [met(joint, 2), met(joint, half + 2)])):
            other = [met(x, 1) for x in same]
            blocks[r] += [same[0], other[0], same[1], other[1]]
    enc_grad, rel_grad = call(
        functools.partial(place_body, buckets), [shaped((feat, emb)), shaped((n_rel, emb))], [*blocks[0], *blocks[1]]
    )
    return (src_grad, tgt_grad, rel_grad, enc_grad)


def solution(mesh):
    in_specs = (
        P(("bucket", "rel"), None),
        P(("bucket", "rel"), None),
        P(),
        P("rel", None),
        P("bucket", "rel", None, None),
        P("bucket", "rel", None, None),
        P("bucket", "rel", None, None, None),
        P("bucket", "rel", None, None),
        P("bucket", "rel", None, None),
    )
    out_specs = (P(("bucket", "rel"), None), P(("bucket", "rel"), None), P("rel", None), P())

    return jax.shard_map(shards, mesh=mesh, in_specs=in_specs, out_specs=out_specs, check_vma=False)
```

```python
import functools

import jax
import jax.numpy as jnp
from jax import lax
from jax.experimental import pallas as pl
from jax.experimental.pallas import tpu as pltpu
from jax.sharding import PartitionSpec as P


CHUNKS = 2
LABELLED = 1024.0
LOG2E = 1.4426950408889634
SLOT_OF = (0, 1, 3, 2)
APART = (0, 2, 1, 3)
NT = (((1,), (1,)), ((), ()))
NN = (((1,), (0,)), ((), ()))
F32 = jnp.float32
BF16 = jnp.bfloat16
VMEM = pl.BlockSpec(memory_space=pltpu.VMEM)
ANY = pl.BlockSpec(memory_space=pl.ANY)


def dot(a, b, dims):
    return lax.dot_general(a, b, dims, preferred_element_type=F32)


def call(body, outs, ins, in_specs=None, scratch=(), flops=0):
    moved = sum(x.size * x.dtype.itemsize for x in ins)
    moved += sum(o.size * o.dtype.itemsize for o in outs)
    return pl.pallas_call(
        body,
        out_shape=tuple(outs),
        in_specs=in_specs or [VMEM] * len(ins),
        out_specs=tuple(VMEM for _ in outs),
        scratch_shapes=scratch,
        cost_estimate=pl.CostEstimate(flops=int(flops), bytes_accessed=int(moved), transcendentals=0),
    )(*ins)


def shaped(shape, dtype=F32):
    return jax.ShapeDtypeStruct(tuple(shape), dtype)


def field_starts(edges, negs):
    starts, at = {}, 0
    for key, size in (
        ("src", edges), ("tlo", edges), ("thi", edges), ("rel", edges), ("lab", edges), ("nlo", negs), ("nhi", negs),
    ):
        starts[key] = (at, size)
        at += size
    return starts, at


def task_rows(edges, negs, width):
    total = field_starts(edges, negs)[1]
    return -(-total // width // 8) * 8 if total % width == 0 else (-(-(-(-total // width)) // 8)) * 8


def pack(fields, rows, src, tgt, rel, neg, lab, flat):
    slots = src.shape[2]
    width = flat.shape[1]
    flat[...] = jnp.zeros_like(flat)
    for m in range(slots):
        tgt_f = tgt[0, 0, m : m + 1, :].astype(F32)
        neg_f = neg[0, 0, m : m + 1, :].astype(F32)
        t_hi = jnp.floor(tgt_f * (1.0 / 256))
        n_hi = jnp.floor(neg_f * (1.0 / 256))
        values = {
            "src": src[0, 0, m : m + 1, :].astype(F32), "tlo": tgt_f - 256.0 * t_hi, "thi": t_hi,
            "rel": rel[m : m + 1, :].astype(F32), "lab": lab[0, 0, m : m + 1, :].astype(F32),
            "nlo": neg_f - 256.0 * n_hi, "nhi": n_hi,
        }
        for key, (at, size) in fields.items():
            done = 0
            while done < size:
                row, col = divmod(at + done, width)
                n = min(width - col, size - done)
                flat[m * rows + row : m * rows + row + 1, col : col + n] = values[key][:, done : done + n]
                done += n


def first_body(fields, rows, src_feat, weight, src, tgt, rel, neg, lab, shift, out, act, flat):
    pack(fields, rows, src, tgt, rel, neg, lab, flat)
    n = src_feat.shape[0]
    value = jnp.tanh(dot(src_feat[...], weight[...], NN))
    act[...] = value
    out[:n, :] = value.astype(BF16)
    tasks = flat.shape[0]
    out[n : n + tasks, :] = flat[...].astype(BF16)
    out[n + tasks :, :] = jnp.zeros_like(out[n + tasks :, :])
    out[n + tasks : n + tasks + shift.shape[0], :] = shift[...]


def take(block, fields, key):
    at, size = fields[key]
    width = block.shape[1]
    pieces, done = [], 0
    while done < size:
        row, col = divmod(at + done, width)
        n = min(width - col, size - done)
        pieces.append(block[row : row + 1, col : col + n])
        done += n
    return pieces[0] if len(pieces) == 1 else jnp.concatenate(pieces, axis=1)


def wrapped(value, base, count):
    moved = value - base
    return jnp.where(moved < 0, moved + count, moved)


def one_hot(rows, ids, value=None):
    one = jnp.full(ids.shape, 1.0, BF16) if value is None else value.astype(BF16)
    pieces = []
    for base in range(0, rows, 256):
        n = min(256, rows - base)
        local = jnp.where((ids >= base) & (ids < base + n), ids - base, -1.0).astype(BF16)
        iota = lax.broadcasted_iota(jnp.int32, (n, ids.shape[1]), 0).astype(F32).astype(BF16)
        pieces.append(jnp.where(iota == local, one, jnp.zeros_like(one)))
    return pieces[0] if len(pieces) == 1 else jnp.concatenate(pieces, axis=0)


def own_quarter(size):
    me = lax.axis_index("bucket")
    return (me & 1) * 2 + ((me >> (size.bit_length() - 2)) & 1)


def own_half():
    return (lax.axis_index("bucket") >> 1) & 1


def aligned(number, size, base=0):
    return pl.ds(pl.multiple_of(base + number * size, size), size)


def prepare_body(size, *refs):
    src, tgt, weight, (act, src_turned, tgt_turned, src_held, tgt_held) = refs[:4], refs[4:8], refs[8], refs[9:]
    me = own_quarter(size)
    for feats, held, turned in ((src, src_held, src_turned), (tgt, tgt_held, tgt_turned)):
        for j, x in enumerate(feats):
            held[aligned(me ^ APART[j], x.shape[0]), :] = x[...]
        turned[...] = held[...].astype(F32).T.astype(BF16)
    act[...] = jnp.tanh(dot(tgt_held[...], weight[:, aligned(me, act.shape[1])], NN))


def spread(pieces, targets):
    own, plus, minus, far_a, far_b = pieces
    copies = []
    half = far_a.shape[0]
    for place, parts in ((0, ((own, 0),)), (1, ((plus, 0),)), (2, ((far_a, 0), (far_b, half))), (3, ((minus, 0),))):
        for lo, hi, ref in targets(place):
            for part, base in parts:
                a, b = max(lo, base), min(hi, base + part.shape[0])
                if a < b:
                    copies.append((part.at[pl.ds(a - base, b - a)], ref.at[pl.ds(a - lo, b - a)]))
    return copies


def weights_of(scores, coded, pairs, scale):
    sig = 1.0 / (1.0 + jnp.exp2(scores * (-scale * LOG2E)))
    labels = jnp.floor(coded * (1.0 / LABELLED))
    edges = coded - (LABELLED - 1.0) * labels
    return edges * sig - labels + pairs * sig.astype(BF16).astype(F32)


def meets_body(cfg, own, plus, minus, far_a, far_b, f_own, f_low, f_high, f_far, weights, *refs):
    fields, rows, s_rows, t_rows, n_rel, scale, groups, negs, size = cfg
    t_outs, s_outs = refs[:4], refs[4:8]
    src, idx, feats, weight_v, tgt, query_a, query_b, parts_a, parts_b, acc, w_src, w_rel, total, sems = refs[8:]
    ring = lax.axis_index("rel")
    tasks = idx.shape[1] - 16

    def places(place):
        return (0, s_rows, src.at[pl.ds(place * s_rows, s_rows)]), (s_rows, own.shape[0], idx.at[place])

    copies = [(weights, weight_v)]
    copies += [(x, feats.at[pl.ds(j * t_rows, t_rows)]) for j, x in enumerate((f_own, f_low, f_high, f_far))]
    early = len(copies)
    copies += spread((own, plus, minus, far_a, far_b), places)
    copies = [pltpu.make_async_copy(a, b, sems.at[i]) for i, (a, b) in enumerate(copies)]
    for c in copies:
        c.start()
    for c in copies[:early]:
        c.wait()
    tgt[...] = jnp.tanh(dot(feats[...], weight_v[...], NN)).astype(BF16)
    for c in copies[early:]:
        c.wait()
    for ref in (acc, w_src, w_rel, query_b, parts_b):
        ref[...] = jnp.zeros_like(ref)
    all_src = src.shape[0]
    all_tgt = t_rows * groups
    src_base = (ring * s_rows).astype(F32)
    tgt_base = (ring * t_rows).astype(F32)
    lane = lax.broadcasted_iota(jnp.int32, (t_rows, w_rel.shape[1]), 1)

    def one_group(group, query, parts):
        shift = idx[group, tasks : tasks + 16, :]
        place = lax.rem(group + ring, groups) * n_rel
        for k in range(n_rel):
            rows_k = src[...] + shift[k : k + 1, :]
            query[k * all_src : (k + 1) * all_src, :] = rows_k
            query[(n_rel + k) * all_src : (n_rel + k + 1) * all_src, :] = rows_k
        scores = dot(tgt[...], query[: n_rel * all_src, :], NT)
        for j, slot in enumerate(SLOT_OF):
            block = idx[group, slot * rows : (slot + 1) * rows, :].astype(F32)
            who = wrapped(take(block, fields, "src"), src_base, float(all_src))
            rel = take(block, fields, "rel")
            ids = wrapped(take(block, fields, "thi") * 256.0 + take(block, fields, "tlo"), tgt_base, float(all_tgt))
            weight = 1.0 + (LABELLED - 1.0) * take(block, fields, "lab")
            left = [one_hot(t_rows, jnp.where(rel == float(k), ids, -1.0), weight) for k in range(n_rel)]
            left.append(one_hot(16, rel))
            counts = dot(jnp.concatenate(left, axis=0), one_hot(all_src, who), NT)
            neg = wrapped(take(block, fields, "nhi") * 256.0 + take(block, fields, "nlo"), tgt_base, float(all_tgt))
            neg_count = jnp.sum(one_hot(t_rows, neg).astype(F32), axis=1, keepdims=True) * (1.0 / negs)
            mine = slice(j * t_rows, (j + 1) * t_rows)
            part, line = None, jnp.zeros((t_rows, w_rel.shape[1]), F32)
            for k in range(n_rel):
                top = k * t_rows
                each = n_rel * t_rows + k
                lanes = slice(k * all_src, (k + 1) * all_src)
                value = weights_of(
                    scores[mine, lanes], counts[top : top + t_rows, :], neg_count * counts[each : each + 1, :], scale
                )
                high = value.astype(BF16)
                parts[mine, lanes] = high
                lanes = slice((n_rel + k) * all_src, (n_rel + k + 1) * all_src)
                parts[mine, lanes] = (value - high.astype(F32)).astype(BF16)
                part = value if part is None else part + value
                line = jnp.where(lane == place + k, jnp.sum(value, axis=1, keepdims=True), line)
            w_src[mine, :] += part
            w_rel[mine, :] += line

    def step(pair, carry):
        one_group(2 * pair, query_a, parts_a)
        acc[...] += dot(parts_b[...], query_b[...], NN)
        one_group(2 * pair + 1, query_b, parts_b)
        acc[...] += dot(parts_a[...], query_a[...], NN)
        return carry

    lax.fori_loop(0, groups // 2, step, 0)
    acc[...] += dot(parts_b[...], query_b[...], NN)
    whole = jnp.concatenate([w_src[...].T, w_rel[...].T[:16, :]], axis=0)
    high = whole.astype(BF16)
    low = (whole - high.astype(F32)).astype(BF16)
    total[...] = scale * (dot(high, tgt[...], NN) + dot(low, tgt[...], NN))
    for r, out in enumerate(s_outs):
        place = lax.rem((ring ^ r) - ring + groups, groups)
        out[...] = total[aligned(place, s_rows), :]
    me = own_quarter(size)
    for i, out in enumerate(t_outs):
        lanes = aligned(me ^ APART[i], out.shape[1])
        for j in range(4):
            out[aligned(me ^ APART[j], t_rows), :] = scale * acc[j * t_rows : (j + 1) * t_rows, lanes]
        out[4 * t_rows :, :] = total[all_src:, lanes]


def source_body(size, a, b, c, d, act, grad, *outs):
    value = (a[...] + b[...]) + (c[...] + d[...])
    grad[...] = value
    d = (value * (1.0 - act[...] * act[...])).astype(BF16)
    wide = outs[0].shape[1]
    me = own_quarter(size)
    for a in range(4):
        for j, out in enumerate(outs):

            @pl.when((me ^ APART[j]) == a)
            def _():
                out[...] = d[:, a * wide : (a + 1) * wide]


def target_body(size, keep, recv, last, act, turned, *outs):
    parts, rows = outs[:2], outs[2:]
    value = (keep[...] + recv[...]) + last[...]
    n = act.shape[0]
    d = (value[:n, :] * (1.0 - act[...] * act[...])).astype(BF16)
    block = turned.shape[0] // 2
    for r, out in enumerate(parts):
        out[:block, :] = dot(turned[aligned(own_half() ^ r, block), :], d, NN)
        out[block:, :] = value[n:, :]
    me = own_quarter(size)
    for a in range(4):
        for j, out in enumerate(rows):

            @pl.when((me ^ APART[j]) == a)
            def _():
                out[...] = value[a * (n // 4) : (a + 1) * (n // 4), :]


def join_body(size, keep_in, send_in, turned, *refs):
    pieces, outs, held = refs[:4], refs[4:-1], refs[-1]
    n = pieces[0].shape[0]
    me = own_quarter(size)
    for j, x in enumerate(pieces):
        held[aligned(me ^ APART[j], n), :] = x[...]
    block = turned.shape[0] // 2
    part = block // CHUNKS
    for r, x in enumerate((keep_in, send_in)):
        added = dot(turned[aligned(own_half() ^ r, block), :], held[...], NN)
        for c, out in enumerate(outs[r * CHUNKS : (r + 1) * CHUNKS]):
            out[:part, :] = x[c * part : (c + 1) * part, :] + added[c * part : (c + 1) * part, :]
            if c == 0:
                out[part:, :] = x[block:, :]


def rows_body(size, *refs):
    parts, (grad,) = refs[:4], refs[4:]
    me = own_quarter(size)
    for j, x in enumerate(parts):
        grad[:, aligned(me ^ APART[j], x.shape[1])] = x[...]


def place_body(size, *refs):
    blocks, (enc_grad, rel_grad) = refs[:-2], refs[-2:]
    part = enc_grad.shape[0] // 2 // CHUNKS
    me = own_quarter(size)
    n_rel = rel_grad.shape[0]
    for at, x in enumerate(blocks):
        r, c, j = at // (4 * CHUNKS), at // 4 % CHUNKS, at % 4
        lanes = aligned(me ^ APART[j], x.shape[1])
        enc_grad[aligned((own_half() ^ r) * CHUNKS + c, part), lanes] = x[:part, :]
        if r == 0 and c == 0:
            for k in range(n_rel):
                rel_grad[k : k + 1, lanes] = x[pl.ds(part + lax.axis_index("rel") * n_rel + k, 1), :]


def shards(src_feat, tgt_feat, enc_weight, rel_shift, edge_src, edge_tgt, rel_hot, neg_idx, edge_label):
    buckets = lax.axis_size("bucket")
    groups = lax.axis_size("rel")
    half = buckets // 2
    s_rows, t_rows = src_feat.shape[0], tgt_feat.shape[0]
    feat, emb = enc_weight.shape
    slots, edges = edge_src.shape[2:]
    negs = neg_idx.shape[3]
    n_rel = rel_hot.shape[3]
    fields, _ = field_starts(edges, negs)
    rows = task_rows(edges, negs, emb)
    cfg = (fields, rows, s_rows, t_rows, n_rel, emb**-0.5, groups, negs, buckets)
    wide = emb // 4

    def met(x, mask):
        return lax.ppermute(x, "bucket", [(i, i ^ mask) for i in range(buckets)])

    def ring(x, step):
        return lax.ppermute(x, "rel", [(i, (i - step) % groups) for i in range(groups)])

    def crossed(x, mask):
        return lax.ppermute(x, "rel", [(i, i ^ mask) for i in range(groups)])

    def around(x):
        cut_at = x.shape[0] // 2
        plus, minus = ring(x, 1), ring(x, -1)
        return x, plus, minus, ring(plus[:cut_at], 1), ring(minus[cut_at:], -1)

    def shared(parts):
        return [parts[0], met(parts[1], 1), met(parts[2], half), met(parts[3], half + 1)]

    which = sum(k * rel_hot[0, 0, :, k, :] for k in range(1, n_rel))
    own, s_act = call(
        functools.partial(first_body, fields, rows),
        [shaped((s_rows + slots * rows + 16, emb), BF16), shaped((s_rows, emb))],
        [src_feat, enc_weight, edge_src, edge_tgt, which, neg_idx, edge_label, rel_shift],
        scratch=[pltpu.VMEM((slots * rows, emb), F32)],
        flops=2 * s_rows * feat * emb,
    )
    first = around(own)

    def fetched(x):
        high = met(x, half)
        return [x, met(x, 1), high, met(high, 1)]

    t_feats, s_feats = fetched(tgt_feat), fetched(src_feat)
    queries = n_rel * groups * s_rows
    t_feats, s_feats = lax.optimization_barrier((t_feats, s_feats))
    parts = call(
        functools.partial(meets_body, cfg),
        [shaped((4 * t_rows + 16, wide))] * 4 + [shaped((s_rows, emb))] * groups,
        [*first, *t_feats, enc_weight],
        in_specs=[ANY] * 10,
        scratch=[
            pltpu.VMEM((groups * s_rows, emb), BF16),
            pltpu.VMEM((groups, slots * rows + 16, emb), BF16),
            pltpu.VMEM((4 * t_rows, feat), BF16),
            pltpu.VMEM((feat, emb), BF16),
            pltpu.VMEM((4 * t_rows, emb), BF16),
            pltpu.VMEM((2 * queries, emb), BF16),
            pltpu.VMEM((2 * queries, emb), BF16),
            pltpu.VMEM((4 * t_rows, 2 * queries), BF16),
            pltpu.VMEM((4 * t_rows, 2 * queries), BF16),
            pltpu.VMEM((4 * t_rows, emb), F32),
            pltpu.VMEM((4 * t_rows, groups * s_rows), F32),
            pltpu.VMEM((4 * t_rows, 128), F32),
            pltpu.VMEM((groups * s_rows + 16, emb), F32),
            pltpu.SemaphoreType.DMA((32,)),
        ],
        flops=12e9,
    )
    t_parts, s_parts = parts[:4], parts[4:]
    s_parts = [s_parts[0], *(crossed(s_parts[mask], mask) for mask in range(1, groups))]
    t_recv, t_next = met(t_parts[1], 1), met(t_parts[3], 1)
    t_last = met(t_parts[2] + t_next, half)
    s_feats, t_recv = lax.optimization_barrier((s_feats, t_recv))
    act, s_turned, t_turned = call(
        functools.partial(prepare_body, buckets),
        [shaped((4 * t_rows, wide)), shaped((feat, 4 * s_rows), BF16), shaped((feat, 4 * t_rows), BF16)],
        [*s_feats, *t_feats, enc_weight],
        scratch=[pltpu.VMEM((4 * s_rows, feat), BF16), pltpu.VMEM((4 * t_rows, feat), BF16)],
        flops=8 * t_rows * feat * wide,
    )
    s_parts, act = lax.optimization_barrier((s_parts, act))
    part = feat // 2
    src_grad, *d_parts = call(
        functools.partial(source_body, buckets),
        [shaped((s_rows, emb))] + [shaped((s_rows, wide), BF16)] * 4,
        [*s_parts, s_act],
    )
    d_parts, t_last = lax.optimization_barrier((d_parts, t_last))
    keep, send, *g_parts = call(
        functools.partial(target_body, buckets),
        [shaped((part + 16, wide))] * 2 + [shaped((t_rows, wide))] * 4,
        [t_parts[0], t_recv, t_last, act, t_turned],
        flops=8 * t_rows * feat * wide,
    )
    d_parts = shared(d_parts)
    piece = part // CHUNKS
    sizes = [shaped((piece + (16 if c == 0 else 0), wide)) for c in range(CHUNKS)] * 2
    halves = call(
        functools.partial(join_body, buckets),
        sizes,
        [keep, send, s_turned, *d_parts],
        scratch=[pltpu.VMEM((4 * s_rows, wide), BF16)],
        flops=8 * s_rows * feat * wide,
    )
    got = [met(x, 2) for x in halves[CHUNKS:]]
    g_parts, got[0] = lax.optimization_barrier((shared(g_parts), got[0]))
    (tgt_grad,) = call(functools.partial(rows_body, buckets), [shaped((t_rows, emb))], g_parts)
    blocks = [[], []]
    for c in range(CHUNKS):
        joint = halves[c] + got[c]
        for bit in range(2, buckets.bit_length() - 2):
            joint = joint + met(joint, 1 << bit)
        for mask in (1, 3) if c % 2 == 0 else (3, 1):
            joint = joint + crossed(joint, mask)
            if c == 0 and mask == 1:
                tgt_grad, joint = lax.optimization_barrier((tgt_grad, joint))
        for r, same in ((0, [joint, met(joint, half)]), (1, [met(joint, 2), met(joint, half + 2)])):
            other = [met(x, 1) for x in same]
            blocks[r] += [same[0], other[0], same[1], other[1]]
    enc_grad, rel_grad = call(
        functools.partial(place_body, buckets), [shaped((feat, emb)), shaped((n_rel, emb))], [*blocks[0], *blocks[1]]
    )
    return (src_grad, tgt_grad, rel_grad, enc_grad)


def solution(mesh):
    in_specs = (
        P(("bucket", "rel"), None),
        P(("bucket", "rel"), None),
        P(),
        P("rel", None),
        P("bucket", "rel", None, None),
        P("bucket", "rel", None, None),
        P("bucket", "rel", None, None, None),
        P("bucket", "rel", None, None),
        P("bucket", "rel", None, None),
    )
    out_specs = (P(("bucket", "rel"), None), P(("bucket", "rel"), None), P("rel", None), P())

    return jax.shard_map(shards, mesh=mesh, in_specs=in_specs, out_specs=out_specs, check_vma=False)
```

```python
import functools

import jax
import jax.numpy as jnp
from jax import lax
from jax.experimental import pallas as pl
from jax.experimental.pallas import tpu as pltpu
from jax.sharding import PartitionSpec as P


CHUNKS = 2
LABELLED = 1024.0
LOG2E = 1.4426950408889634
SLOT_OF = (0, 1, 3, 2)
APART = (0, 2, 1, 3)
NT = (((1,), (1,)), ((), ()))
NN = (((1,), (0,)), ((), ()))
F32 = jnp.float32
BF16 = jnp.bfloat16
VMEM = pl.BlockSpec(memory_space=pltpu.VMEM)
ANY = pl.BlockSpec(memory_space=pl.ANY)


def dot(a, b, dims):
    return lax.dot_general(a, b, dims, preferred_element_type=F32)


def call(body, outs, ins, in_specs=None, scratch=(), flops=0):
    moved = sum(x.size * x.dtype.itemsize for x in ins)
    moved += sum(o.size * o.dtype.itemsize for o in outs)
    return pl.pallas_call(
        body,
        out_shape=tuple(outs),
        in_specs=in_specs or [VMEM] * len(ins),
        out_specs=tuple(VMEM for _ in outs),
        scratch_shapes=scratch,
        cost_estimate=pl.CostEstimate(flops=int(flops), bytes_accessed=int(moved), transcendentals=0),
    )(*ins)


def shaped(shape, dtype=F32):
    return jax.ShapeDtypeStruct(tuple(shape), dtype)


def field_starts(edges, negs):
    starts, at = {}, 0
    for key, size in (
        ("src", edges), ("tlo", edges), ("thi", edges), ("rel", edges), ("lab", edges), ("nlo", negs), ("nhi", negs),
    ):
        starts[key] = (at, size)
        at += size
    return starts, at


def task_rows(edges, negs, width):
    total = field_starts(edges, negs)[1]
    return -(-total // width // 8) * 8 if total % width == 0 else (-(-(-(-total // width)) // 8)) * 8


def pack(fields, rows, src, tgt, rel, neg, lab, flat):
    slots = src.shape[2]
    width = flat.shape[1]
    flat[...] = jnp.zeros_like(flat)
    for m in range(slots):
        tgt_f = tgt[0, 0, m : m + 1, :].astype(F32)
        neg_f = neg[0, 0, m : m + 1, :].astype(F32)
        t_hi = jnp.floor(tgt_f * (1.0 / 256))
        n_hi = jnp.floor(neg_f * (1.0 / 256))
        values = {
            "src": src[0, 0, m : m + 1, :].astype(F32), "tlo": tgt_f - 256.0 * t_hi, "thi": t_hi,
            "rel": rel[m : m + 1, :].astype(F32), "lab": lab[0, 0, m : m + 1, :].astype(F32),
            "nlo": neg_f - 256.0 * n_hi, "nhi": n_hi,
        }
        for key, (at, size) in fields.items():
            done = 0
            while done < size:
                row, col = divmod(at + done, width)
                n = min(width - col, size - done)
                flat[m * rows + row : m * rows + row + 1, col : col + n] = values[key][:, done : done + n]
                done += n


def first_body(fields, rows, src_feat, weight, src, tgt, rel, neg, lab, shift, out, act, flat):
    pack(fields, rows, src, tgt, rel, neg, lab, flat)
    n = src_feat.shape[0]
    value = jnp.tanh(dot(src_feat[...], weight[...], NN))
    act[...] = value
    out[:n, :] = value.astype(BF16)
    tasks = flat.shape[0]
    out[n : n + tasks, :] = flat[...].astype(BF16)
    out[n + tasks :, :] = jnp.zeros_like(out[n + tasks :, :])
    out[n + tasks : n + tasks + shift.shape[0], :] = shift[...]


def take(block, fields, key):
    at, size = fields[key]
    width = block.shape[1]
    pieces, done = [], 0
    while done < size:
        row, col = divmod(at + done, width)
        n = min(width - col, size - done)
        pieces.append(block[row : row + 1, col : col + n])
        done += n
    return pieces[0] if len(pieces) == 1 else jnp.concatenate(pieces, axis=1)


def wrapped(value, base, count):
    moved = value - base
    return jnp.where(moved < 0, moved + count, moved)


def one_hot(rows, ids, value=None):
    one = jnp.full(ids.shape, 1.0, BF16) if value is None else value.astype(BF16)
    pieces = []
    for base in range(0, rows, 256):
        n = min(256, rows - base)
        local = jnp.where((ids >= base) & (ids < base + n), ids - base, -1.0).astype(BF16)
        iota = lax.broadcasted_iota(jnp.int32, (n, ids.shape[1]), 0).astype(F32).astype(BF16)
        pieces.append(jnp.where(iota == local, one, jnp.zeros_like(one)))
    return pieces[0] if len(pieces) == 1 else jnp.concatenate(pieces, axis=0)


def own_quarter(size):
    me = lax.axis_index("bucket")
    return (me & 1) * 2 + ((me >> (size.bit_length() - 2)) & 1)


def own_half():
    return (lax.axis_index("bucket") >> 1) & 1


def aligned(number, size, base=0):
    return pl.ds(pl.multiple_of(base + number * size, size), size)


def prepare_body(size, *refs):
    src, tgt, weight, (act, src_turned, tgt_turned, src_held, tgt_held, columns, sems) = refs[:4], refs[4:8], refs[8], refs[9:]
    me = own_quarter(size)
    copies = [(weight.at[:, aligned(me, act.shape[1])], columns)]
    for feats, held in ((src, src_held), (tgt, tgt_held)):
        copies += [(x, held.at[aligned(me ^ APART[j], x.shape[0])]) for j, x in enumerate(feats)]
    start_all(copies, sems)
    for held, turned in ((src_held, src_turned), (tgt_held, tgt_turned)):
        turned[...] = held[...].astype(F32).T.astype(BF16)
    act[...] = jnp.tanh(dot(tgt_held[...], columns[...], NN))


def start_all(copies, sems):
    started = [pltpu.make_async_copy(a, b, sems.at[i]) for i, (a, b) in enumerate(copies)]
    for c in started:
        c.start()
    for c in started:
        c.wait()


def spread(pieces, targets):
    own, plus, minus, far_a, far_b = pieces
    copies = []
    half = far_a.shape[0]
    for place, parts in ((0, ((own, 0),)), (1, ((plus, 0),)), (2, ((far_a, 0), (far_b, half))), (3, ((minus, 0),))):
        for lo, hi, ref in targets(place):
            for part, base in parts:
                a, b = max(lo, base), min(hi, base + part.shape[0])
                if a < b:
                    copies.append((part.at[pl.ds(a - base, b - a)], ref.at[pl.ds(a - lo, b - a)]))
    return copies


def weights_of(scores, coded, pairs, scale):
    sig = 1.0 / (1.0 + jnp.exp2(scores * (-scale * LOG2E)))
    labels = jnp.floor(coded * (1.0 / LABELLED))
    edges = coded - (LABELLED - 1.0) * labels
    return edges * sig - labels + pairs * sig.astype(BF16).astype(F32)


def meets_body(cfg, own, plus, minus, far_a, far_b, f_own, f_low, f_high, f_far, weights, *refs):
    fields, rows, s_rows, t_rows, n_rel, scale, groups, negs, size = cfg
    t_outs, s_outs = refs[:4], refs[4:8]
    src, idx, feats, weight_v, tgt, query_a, query_b, parts_a, parts_b, acc, w_src, w_rel, total, sems = refs[8:]
    ring = lax.axis_index("rel")
    tasks = idx.shape[1] - 16

    def places(place):
        return (0, s_rows, src.at[pl.ds(place * s_rows, s_rows)]), (s_rows, own.shape[0], idx.at[place])

    copies = [(weights, weight_v)]
    copies += [(x, feats.at[pl.ds(j * t_rows, t_rows)]) for j, x in enumerate((f_own, f_low, f_high, f_far))]
    early = len(copies)
    copies += spread((own, plus, minus, far_a, far_b), places)
    copies = [pltpu.make_async_copy(a, b, sems.at[i]) for i, (a, b) in enumerate(copies)]
    for c in copies:
        c.start()
    for c in copies[:early]:
        c.wait()
    tgt[...] = jnp.tanh(dot(feats[...], weight_v[...], NN)).astype(BF16)
    for c in copies[early:]:
        c.wait()
    for ref in (acc, w_src, w_rel, query_b, parts_b):
        ref[...] = jnp.zeros_like(ref)
    all_src = src.shape[0]
    all_tgt = t_rows * groups
    src_base = (ring * s_rows).astype(F32)
    tgt_base = (ring * t_rows).astype(F32)
    lane = lax.broadcasted_iota(jnp.int32, (t_rows, w_rel.shape[1]), 1)

    def one_group(group, query, parts):
        shift = idx[group, tasks : tasks + 16, :]
        place = lax.rem(group + ring, groups) * n_rel
        for k in range(n_rel):
            rows_k = src[...] + shift[k : k + 1, :]
            query[k * all_src : (k + 1) * all_src, :] = rows_k
            query[(n_rel + k) * all_src : (n_rel + k + 1) * all_src, :] = rows_k
        scores = dot(tgt[...], query[: n_rel * all_src, :], NT)
        for j, slot in enumerate(SLOT_OF):
            block = idx[group, slot * rows : (slot + 1) * rows, :].astype(F32)
            who = wrapped(take(block, fields, "src"), src_base, float(all_src))
            rel = take(block, fields, "rel")
            ids = wrapped(take(block, fields, "thi") * 256.0 + take(block, fields, "tlo"), tgt_base, float(all_tgt))
            weight = 1.0 + (LABELLED - 1.0) * take(block, fields, "lab")
            left = [one_hot(t_rows, jnp.where(rel == float(k), ids, -1.0), weight) for k in range(n_rel)]
            left.append(one_hot(16, rel))
            counts = dot(jnp.concatenate(left, axis=0), one_hot(all_src, who), NT)
            neg = wrapped(take(block, fields, "nhi") * 256.0 + take(block, fields, "nlo"), tgt_base, float(all_tgt))
            neg_count = jnp.sum(one_hot(t_rows, neg).astype(F32), axis=1, keepdims=True) * (1.0 / negs)
            mine = slice(j * t_rows, (j + 1) * t_rows)
            part, line = None, jnp.zeros((t_rows, w_rel.shape[1]), F32)
            for k in range(n_rel):
                top = k * t_rows
                each = n_rel * t_rows + k
                lanes = slice(k * all_src, (k + 1) * all_src)
                value = weights_of(
                    scores[mine, lanes], counts[top : top + t_rows, :], neg_count * counts[each : each + 1, :], scale
                )
                high = value.astype(BF16)
                parts[mine, lanes] = high
                lanes = slice((n_rel + k) * all_src, (n_rel + k + 1) * all_src)
                parts[mine, lanes] = (value - high.astype(F32)).astype(BF16)
                part = value if part is None else part + value
                line = jnp.where(lane == place + k, jnp.sum(value, axis=1, keepdims=True), line)
            w_src[mine, :] += part
            w_rel[mine, :] += line

    def step(pair, carry):
        one_group(2 * pair, query_a, parts_a)
        acc[...] += dot(parts_b[...], query_b[...], NN)
        one_group(2 * pair + 1, query_b, parts_b)
        acc[...] += dot(parts_a[...], query_a[...], NN)
        return carry

    lax.fori_loop(0, groups // 2, step, 0)
    acc[...] += dot(parts_b[...], query_b[...], NN)
    whole = jnp.concatenate([w_src[...].T, w_rel[...].T[:16, :]], axis=0)
    high = whole.astype(BF16)
    low = (whole - high.astype(F32)).astype(BF16)
    total[...] = scale * (dot(high, tgt[...], NN) + dot(low, tgt[...], NN))
    for r, out in enumerate(s_outs):
        place = lax.rem((ring ^ r) - ring + groups, groups)
        out[...] = total[aligned(place, s_rows), :]
    me = own_quarter(size)
    for i, out in enumerate(t_outs):
        lanes = aligned(me ^ APART[i], out.shape[1])
        for j in range(4):
            out[aligned(me ^ APART[j], t_rows), :] = scale * acc[j * t_rows : (j + 1) * t_rows, lanes]
        out[4 * t_rows :, :] = total[all_src:, lanes]


def source_body(size, a, b, c, d, act, grad, *outs):
    value = (a[...] + b[...]) + (c[...] + d[...])
    grad[...] = value
    d = (value * (1.0 - act[...] * act[...])).astype(BF16)
    wide = outs[0].shape[1]
    me = own_quarter(size)
    for a in range(4):
        for j, out in enumerate(outs):

            @pl.when((me ^ APART[j]) == a)
            def _():
                out[...] = d[:, a * wide : (a + 1) * wide]


def target_body(size, keep, recv, last, act, turned, *outs):
    parts, rows = outs[:2], outs[2:]
    value = (keep[...] + recv[...]) + last[...]
    n = act.shape[0]
    d = (value[:n, :] * (1.0 - act[...] * act[...])).astype(BF16)
    block = turned.shape[0] // 2
    for r, out in enumerate(parts):
        out[:block, :] = dot(turned[aligned(own_half() ^ r, block), :], d, NN)
        out[block:, :] = value[n:, :]
    me = own_quarter(size)
    for a in range(4):
        for j, out in enumerate(rows):

            @pl.when((me ^ APART[j]) == a)
            def _():
                out[...] = value[a * (n // 4) : (a + 1) * (n // 4), :]


def join_body(size, keep_in, send_in, turned, *refs):
    pieces, outs, held = refs[:4], refs[4:-1], refs[-1]
    n = pieces[0].shape[0]
    me = own_quarter(size)
    for j, x in enumerate(pieces):
        held[aligned(me ^ APART[j], n), :] = x[...]
    block = turned.shape[0] // 2
    part = block // CHUNKS
    for r, x in enumerate((keep_in, send_in)):
        added = dot(turned[aligned(own_half() ^ r, block), :], held[...], NN)
        for c, out in enumerate(outs[r * CHUNKS : (r + 1) * CHUNKS]):
            out[:part, :] = x[c * part : (c + 1) * part, :] + added[c * part : (c + 1) * part, :]
            if c == 0:
                out[part:, :] = x[block:, :]


def rows_body(size, *refs):
    parts, (grad,) = refs[:4], refs[4:]
    me = own_quarter(size)
    for j, x in enumerate(parts):
        grad[:, aligned(me ^ APART[j], x.shape[1])] = x[...]


def place_body(size, *refs):
    blocks, (enc_grad, rel_grad) = refs[:-2], refs[-2:]
    part = enc_grad.shape[0] // 2 // CHUNKS
    me = own_quarter(size)
    n_rel = rel_grad.shape[0]
    for at, x in enumerate(blocks):
        r, c, j = at // (4 * CHUNKS), at // 4 % CHUNKS, at % 4
        lanes = aligned(me ^ APART[j], x.shape[1])
        enc_grad[aligned((own_half() ^ r) * CHUNKS + c, part), lanes] = x[:part, :]
        if r == 0 and c == 0:
            for k in range(n_rel):
                rel_grad[k : k + 1, lanes] = x[pl.ds(part + lax.axis_index("rel") * n_rel + k, 1), :]


def shards(src_feat, tgt_feat, enc_weight, rel_shift, edge_src, edge_tgt, rel_hot, neg_idx, edge_label):
    buckets = lax.axis_size("bucket")
    groups = lax.axis_size("rel")
    half = buckets // 2
    s_rows, t_rows = src_feat.shape[0], tgt_feat.shape[0]
    feat, emb = enc_weight.shape
    slots, edges = edge_src.shape[2:]
    negs = neg_idx.shape[3]
    n_rel = rel_hot.shape[3]
    fields, _ = field_starts(edges, negs)
    rows = task_rows(edges, negs, emb)
    cfg = (fields, rows, s_rows, t_rows, n_rel, emb**-0.5, groups, negs, buckets)
    wide = emb // 4

    def met(x, mask):
        return lax.ppermute(x, "bucket", [(i, i ^ mask) for i in range(buckets)])

    def ring(x, step):
        return lax.ppermute(x, "rel", [(i, (i - step) % groups) for i in range(groups)])

    def crossed(x, mask):
        return lax.ppermute(x, "rel", [(i, i ^ mask) for i in range(groups)])

    def around(x):
        cut_at = x.shape[0] // 2
        plus, minus = ring(x, 1), ring(x, -1)
        return x, plus, minus, ring(plus[:cut_at], 1), ring(minus[cut_at:], -1)

    def shared(parts):
        return [parts[0], met(parts[1], 1), met(parts[2], half), met(parts[3], half + 1)]

    which = sum(k * rel_hot[0, 0, :, k, :] for k in range(1, n_rel))
    own, s_act = call(
        functools.partial(first_body, fields, rows),
        [shaped((s_rows + slots * rows + 16, emb), BF16), shaped((s_rows, emb))],
        [src_feat, enc_weight, edge_src, edge_tgt, which, neg_idx, edge_label, rel_shift],
        scratch=[pltpu.VMEM((slots * rows, emb), F32)],
        flops=2 * s_rows * feat * emb,
    )
    first = around(own)

    def fetched(x):
        high = met(x, half)
        return [x, met(x, 1), high, met(high, 1)]

    t_feats, s_feats = fetched(tgt_feat), fetched(src_feat)
    queries = n_rel * groups * s_rows
    t_feats, s_feats = lax.optimization_barrier((t_feats, s_feats))
    parts = call(
        functools.partial(meets_body, cfg),
        [shaped((4 * t_rows + 16, wide))] * 4 + [shaped((s_rows, emb))] * groups,
        [*first, *t_feats, enc_weight],
        in_specs=[ANY] * 10,
        scratch=[
            pltpu.VMEM((groups * s_rows, emb), BF16),
            pltpu.VMEM((groups, slots * rows + 16, emb), BF16),
            pltpu.VMEM((4 * t_rows, feat), BF16),
            pltpu.VMEM((feat, emb), BF16),
            pltpu.VMEM((4 * t_rows, emb), BF16),
            pltpu.VMEM((2 * queries, emb), BF16),
            pltpu.VMEM((2 * queries, emb), BF16),
            pltpu.VMEM((4 * t_rows, 2 * queries), BF16),
            pltpu.VMEM((4 * t_rows, 2 * queries), BF16),
            pltpu.VMEM((4 * t_rows, emb), F32),
            pltpu.VMEM((4 * t_rows, groups * s_rows), F32),
            pltpu.VMEM((4 * t_rows, 128), F32),
            pltpu.VMEM((groups * s_rows + 16, emb), F32),
            pltpu.SemaphoreType.DMA((32,)),
        ],
        flops=12e9,
    )
    t_parts, s_parts = parts[:4], parts[4:]
    s_parts = [s_parts[0], *(crossed(s_parts[mask], mask) for mask in range(1, groups))]
    t_recv, t_next = met(t_parts[1], 1), met(t_parts[3], 1)
    t_last = met(t_parts[2] + t_next, half)
    s_feats, t_recv = lax.optimization_barrier((s_feats, t_recv))
    act, s_turned, t_turned = call(
        functools.partial(prepare_body, buckets),
        [shaped((4 * t_rows, wide)), shaped((feat, 4 * s_rows), BF16), shaped((feat, 4 * t_rows), BF16)],
        [*s_feats, *t_feats, enc_weight],
        in_specs=[ANY] * 9,
        scratch=[
            pltpu.VMEM((4 * s_rows, feat), BF16),
            pltpu.VMEM((4 * t_rows, feat), BF16),
            pltpu.VMEM((feat, wide), BF16),
            pltpu.SemaphoreType.DMA((9,)),
        ],
        flops=8 * t_rows * feat * wide,
    )
    s_parts, act = lax.optimization_barrier((s_parts, act))
    part = feat // 2
    src_grad, *d_parts = call(
        functools.partial(source_body, buckets),
        [shaped((s_rows, emb))] + [shaped((s_rows, wide), BF16)] * 4,
        [*s_parts, s_act],
    )
    d_parts, t_last = lax.optimization_barrier((d_parts, t_last))
    keep, send, *g_parts = call(
        functools.partial(target_body, buckets),
        [shaped((part + 16, wide))] * 2 + [shaped((t_rows, wide))] * 4,
        [t_parts[0], t_recv, t_last, act, t_turned],
        flops=8 * t_rows * feat * wide,
    )
    d_parts = shared(d_parts)
    piece = part // CHUNKS
    sizes = [shaped((piece + (16 if c == 0 else 0), wide)) for c in range(CHUNKS)] * 2
    halves = call(
        functools.partial(join_body, buckets),
        sizes,
        [keep, send, s_turned, *d_parts],
        scratch=[pltpu.VMEM((4 * s_rows, wide), BF16)],
        flops=8 * s_rows * feat * wide,
    )
    got = [met(x, 2) for x in halves[CHUNKS:]]
    g_parts, got[0] = lax.optimization_barrier((shared(g_parts), got[0]))
    (tgt_grad,) = call(functools.partial(rows_body, buckets), [shaped((t_rows, emb))], g_parts)
    blocks = [[], []]
    for c in range(CHUNKS):
        joint = halves[c] + got[c]
        for bit in range(2, buckets.bit_length() - 2):
            joint = joint + met(joint, 1 << bit)
        for mask in (1, 3) if c % 2 == 0 else (3, 1):
            joint = joint + crossed(joint, mask)
            if c == 0 and mask == 1:
                tgt_grad, joint = lax.optimization_barrier((tgt_grad, joint))
        for r, same in ((0, [joint, met(joint, half)]), (1, [met(joint, 2), met(joint, half + 2)])):
            other = [met(x, 1) for x in same]
            blocks[r] += [same[0], other[0], same[1], other[1]]
    enc_grad, rel_grad = call(
        functools.partial(place_body, buckets), [shaped((feat, emb)), shaped((n_rel, emb))], [*blocks[0], *blocks[1]]
    )
    return (src_grad, tgt_grad, rel_grad, enc_grad)


def solution(mesh):
    in_specs = (
        P(("bucket", "rel"), None),
        P(("bucket", "rel"), None),
        P(),
        P("rel", None),
        P("bucket", "rel", None, None),
        P("bucket", "rel", None, None),
        P("bucket", "rel", None, None, None),
        P("bucket", "rel", None, None),
        P("bucket", "rel", None, None),
    )
    out_specs = (P(("bucket", "rel"), None), P(("bucket", "rel"), None), P("rel", None), P())

    return jax.shard_map(shards, mesh=mesh, in_specs=in_specs, out_specs=out_specs, check_vma=False)
```
